32 devices in a mesh: expert: 8 (over z, y), dp: 4 (over x, core).
Axes of the slice: x: 2, y: 2, z: 4, core: 2. Of those that a mesh axis runs over, the one named last changes fastest.
Arguments:
- tokens: bfloat16 [4096, 1440], P(('expert', 'dp')), may hold values from -6 to 6
- routes: int32 [4096, 4], P(('expert', 'dp')), may hold values from 0 to 7, as said below
- gate_fixed: int32 [4096, 4], P(('expert', 'dp')), may hold values from 4096 to 65535
- counts: int32 [32], P(('expert', 'dp')), may hold values from 32 to 128, as said below
- replica_plan: int32 [4], replicated, may hold values from 0 to 7, as said below
- weight_in: bfloat16 [8, 1440, 1440], P('expert', None, 'dp'), may hold values from -0.15625 to 0.15625
- weight_out: bfloat16 [8, 1440, 1440], P('expert', 'dp'), may hold values from -0.15625 to 0.15625
- cotangent: bfloat16 [4096, 1440], P(('expert', 'dp')), may hold values from -0.59765625 to 0.59765625
Outputs:
- layer_output: bfloat16 [4096, 1440], P(('expert', 'dp'))
- input_grads: bfloat16 [4096, 1440], P(('expert', 'dp'))
- weight_in_grad: bfloat16 [8, 1440, 1440], P('expert', None, 'dp')
- weight_out_grad: bfloat16 [8, 1440, 1440], P('expert', 'dp')
The draws below stay inside these ranges and needn't reach their ends.
Inputs may be any that keep to these rules, and one draw needn't show every extreme that they name: `routes`: each row names 4 different experts. `replica_plan`: 4 different experts, among them 0, 3, 4 and 7, in any order. `counts`: some device has 128 live tokens in every draw.
All inputs are finite; a program needn't handle non-finite values.
Results may differ from the reference program's by a relative error of at most 0.0064.
Values may be sent and summed in bfloat16 or wider, within the bound.
A program may use at most 128 MiB of HBM per device.

```python
import jax
import jax.numpy as jnp
from jax import lax

D = 1440
FF = 1440
PATHS_EACH_WORD = 4
TOK_DEV = 128
SPECIALIST_NUM = 8
WORD_SUM = 4096
HOT = 4
CAP = 24
SPARE = 12
DEVICES = 32


def hot_experts(key):
    half_experts = SPECIALIST_NUM // 2
    expert_ids = jnp.arange(SPECIALIST_NUM, dtype=jnp.int32)
    pinned = ((expert_ids == 0) | (expert_ids == half_experts - 1) | (expert_ids == half_experts) | (expert_ids == SPECIALIST_NUM - 1)).astype(jnp.int32)
    priority = jax.random.permutation(jax.random.fold_in(key, 71), SPECIALIST_NUM).astype(jnp.int32)
    scores = priority + pinned * SPECIALIST_NUM
    chosen_scores, chosen = lax.top_k(scores, HOT)
    order = jax.random.permutation(jax.random.fold_in(key, 72), HOT).astype(jnp.int32)
    return chosen.astype(jnp.int32)[order].astype(jnp.int32)


def draw_replica_plan(key, part):
    return hot_experts(key)


def draw_routes(key, part):
    hot_list = hot_experts(key)
    frequent_indicator = jnp.sum((hot_list[:, None] == jnp.arange(SPECIALIST_NUM, dtype=jnp.int32)[None, :]).astype(jnp.int32), axis=0)
    unboosted_logit = jax.random.randint(jax.random.fold_in(key, 73), (WORD_SUM, SPECIALIST_NUM), 0, 1024, dtype=jnp.int32)
    frequent_uplift = (jax.random.randint(jax.random.fold_in(key, 74), (WORD_SUM, SPECIALIST_NUM), 0, SPECIALIST_NUM, dtype=jnp.int32) < 2 * PATHS_EACH_WORD).astype(jnp.int32) * frequent_indicator[None, :]
    specialist_logits = (unboosted_logit + 1024 * frequent_uplift) * SPECIALIST_NUM + jnp.arange(SPECIALIST_NUM, dtype=jnp.int32)[None, :]
    chosen_values, chosen = lax.top_k(specialist_logits, PATHS_EACH_WORD)
    return chosen.astype(jnp.int32)


def draw_counts(key, part):
    values = jax.random.randint(key, (DEVICES,), TOK_DEV // 4, TOK_DEV + 1, dtype=jnp.int32)
    chosen = jax.random.randint(jax.random.fold_in(key, 11), (), 0, DEVICES, dtype=jnp.int32)
    return jnp.where(jnp.arange(DEVICES, dtype=jnp.int32) == chosen, TOK_DEV, values).astype(jnp.int32)


def with_ends(drawn, own_key, low, high):
    extent = drawn.shape
    spot = [jax.random.randint(jax.random.fold_in(own_key, axis), (), 0, extent[axis]) for axis in range(len(extent))]
    drawn = drawn.at[tuple(spot)].set(low)
    longest = extent.index(max(extent))
    spot[longest] = (spot[longest] + 1) % extent[longest]
    return drawn.at[tuple(spot)].set(high)


def level_of(stream_key, shape, pieces, least, largest):
    loudness, own = 1.0, jax.random.fold_in(stream_key, 6)
    for dim, blocks in pieces:
        steps = jnp.exp(jax.random.uniform(jax.random.fold_in(own, dim), (blocks,), jnp.float32, least / len(pieces), largest / len(pieces)))
        loudness = loudness * jnp.repeat(steps, shape[dim] // blocks).reshape([-1 if axis == dim else 1 for axis in range(len(shape))])
    return loudness


def noise(key, extent, deviation, most, pieces=(), kind=jnp.bfloat16):
    result = deviation * jax.random.normal(key, extent, jnp.float32)
    if pieces:
        result = result * level_of(key, extent, pieces, -0.22, 0.18)
    return jnp.clip(result, -most, most).astype(kind)


def setup_inputs(seed: int = 0) -> dict:
    arg_keys = jax.random.split(jax.random.key(seed), 9)
    return {
        "tokens": noise(arg_keys[0], (WORD_SUM, D), 1.0, 6.0, ((0, 32),)),
        "routes": draw_routes(jax.random.fold_in(arg_keys[8], 71), 0),
        "gate_fixed": with_ends(jax.random.randint(arg_keys[2], (WORD_SUM, PATHS_EACH_WORD), 4096, 65536), jax.random.fold_in(arg_keys[2], 1), 4096, 65535).astype(jnp.int32),
        "counts": draw_counts(jax.random.fold_in(arg_keys[8], 71), 0),
        "replica_plan": draw_replica_plan(jax.random.fold_in(arg_keys[8], 71), 0),
        "weight_in": noise(arg_keys[5], (SPECIALIST_NUM, D, FF), D ** -0.5, 0.15625, ((0, 8), (2, 4))),
        "weight_out": noise(arg_keys[6], (SPECIALIST_NUM, FF, D), FF ** -0.5, 0.15625, ((0, 8), (1, 4))),
        "cotangent": noise(arg_keys[7], (WORD_SUM, D), 0.1, 0.59765625, ((0, 32),)),
    }


def activate(values):
    return values * jax.nn.sigmoid(1.702 * values)


def derivative(values):
    sigmoid_value = jax.nn.sigmoid(1.702 * values)
    return sigmoid_value + 1.702 * values * sigmoid_value * (1.0 - sigmoid_value)


def slot_tables(routes, live_count, frequent_indicator, experts, capacity, spare_slots):
    token_count, top_count = routes.shape
    slot_width = capacity + spare_slots
    active = (jnp.arange(token_count, dtype=jnp.int32) < live_count).astype(jnp.int32)
    flattened = routes.reshape(-1).astype(jnp.int32)
    active_flat = jnp.repeat(active, top_count, total_repeat_length=token_count * top_count)
    same_expert = (flattened[:, None] == jnp.arange(experts, dtype=jnp.int32)[None, :]).astype(jnp.int32)
    matches = same_expert * active_flat[:, None]
    before = jnp.cumsum(matches, axis=0) - matches
    position = jnp.sum(before * matches, axis=1).astype(jnp.int32)
    hot_route = jnp.sum(same_expert * frequent_indicator[None, :], axis=1).astype(jnp.int32)
    keep_route = (active_flat > 0) & (position < capacity + spare_slots * hot_route)
    target_block = jnp.where(position < capacity, flattened, (flattened + experts // 2) % experts).astype(jnp.int32)
    slot_index = jnp.where(keep_route, target_block * slot_width + position, experts * slot_width).astype(jnp.int32)
    source = jnp.full((experts * slot_width + 1,), -1, jnp.int32)
    source = source.at[slot_index].set(jnp.arange(token_count * top_count, dtype=jnp.int32))
    return slot_index, source[:experts * slot_width]


def reference(tokens, routes, gate_fixed, counts, replica_plan, weight_in, weight_out, cotangent):
    devices = counts.shape[0]
    slot_width = CAP + SPARE
    frequent_indicator = jnp.sum((replica_plan[:, None] == jnp.arange(SPECIALIST_NUM, dtype=jnp.int32)[None, :]).astype(jnp.int32), axis=0).astype(jnp.int32)
    per_device = routes.reshape(devices, TOK_DEV, PATHS_EACH_WORD)
    slot_all, source_all = jax.vmap(lambda block_routes, live_count: slot_tables(block_routes, live_count, frequent_indicator, SPECIALIST_NUM, CAP, SPARE))(per_device, counts)
    offsets = (jnp.arange(devices, dtype=jnp.int32) * (TOK_DEV * PATHS_EACH_WORD))[:, None]
    global_ids = jnp.where(source_all >= 0, source_all + offsets, -1).astype(jnp.int32).reshape(devices, SPECIALIST_NUM, slot_width)
    partner = ((jnp.arange(SPECIALIST_NUM, dtype=jnp.int32) + SPECIALIST_NUM // 2) % SPECIALIST_NUM).astype(jnp.int32)
    expert_ids = jnp.concatenate([global_ids[:, :, :CAP], global_ids[:, partner, CAP:]], axis=2)
    expert_ids = expert_ids.transpose(1, 0, 2).reshape(SPECIALIST_NUM, devices * slot_width)
    scales = gate_fixed.reshape(-1).astype(jnp.float32) / 65536.0

    def per_expert(expert):
        route_ids = expert_ids[expert]
        filled = (route_ids >= 0)[:, None]
        clipped = jnp.maximum(route_ids, 0).astype(jnp.int32)
        token_ids = (clipped // PATHS_EACH_WORD).astype(jnp.int32)
        inputs = jnp.where(filled, tokens[token_ids], jnp.zeros((), tokens.dtype))
        grad_rows = jnp.where(filled, scales[clipped][:, None] * cotangent[token_ids].astype(jnp.float32), 0.0).astype(jnp.bfloat16)
        w_first = weight_in[expert]
        w_second = weight_out[expert]
        preact = jnp.dot(inputs, w_first, preferred_element_type=jnp.float32)
        activation = activate(preact).astype(jnp.bfloat16)
        outputs = jnp.dot(activation, w_second, preferred_element_type=jnp.float32).astype(jnp.bfloat16)
        act_grad = jnp.dot(grad_rows, w_second.T, preferred_element_type=jnp.float32)
        pre_grad = (act_grad * derivative(preact)).astype(jnp.bfloat16)
        input_rows = jnp.dot(pre_grad, w_first.T, preferred_element_type=jnp.float32).astype(jnp.bfloat16)
        grad_first = jnp.dot(inputs.T, pre_grad, preferred_element_type=jnp.float32).astype(jnp.bfloat16)
        grad_second = jnp.dot(activation.T, grad_rows, preferred_element_type=jnp.float32).astype(jnp.bfloat16)
        return outputs, input_rows, grad_first, grad_second

    outputs, input_rows, grad_first, grad_second = lax.map(per_expert, jnp.arange(SPECIALIST_NUM, dtype=jnp.int32))
    targets = jnp.where(expert_ids >= 0, expert_ids, WORD_SUM * PATHS_EACH_WORD).astype(jnp.int32).reshape(-1)
    route_out = jnp.zeros((WORD_SUM * PATHS_EACH_WORD + 1, D), outputs.dtype).at[targets].set(outputs.reshape(-1, D))[:-1]
    route_dx = jnp.zeros((WORD_SUM * PATHS_EACH_WORD + 1, D), input_rows.dtype).at[targets].set(input_rows.reshape(-1, D))[:-1]
    weighted = route_out.astype(jnp.float32) * scales[:, None]
    layer_output = jnp.sum(weighted.reshape(WORD_SUM, PATHS_EACH_WORD, D), axis=1).astype(jnp.bfloat16)
    input_grads = jnp.sum(route_dx.astype(jnp.float32).reshape(WORD_SUM, PATHS_EACH_WORD, D), axis=1).astype(jnp.bfloat16)
    return layer_output, input_grads, grad_first, grad_second
```

```python
import jax
import jax.numpy as jnp
from jax import lax
from jax.sharding import PartitionSpec as P

F32 = jnp.float32
BF16 = jnp.bfloat16


def activate(values):
    return values * jax.nn.sigmoid(1.702 * values)


def derivative(values):
    s = jax.nn.sigmoid(1.702 * values)
    return s + 1.702 * values * s * (1.0 - s)


def dot(a, b, dims):
    return lax.dot_general(a, b, (dims, ((), ())), preferred_element_type=F32)


def tables(routes, gate_fixed, live_count, plan, experts, capacity, spare):
    tokens = routes.shape[0]
    width = capacity + spare
    ids = jnp.arange(experts, dtype=jnp.int32)
    live = (jnp.arange(tokens, dtype=jnp.int32) < live_count)[:, None]
    same = routes[:, :, None] == ids[None, None, :]
    member = jnp.any(same, axis=1) & live
    gate = jnp.sum(jnp.where(same, gate_fixed[:, :, None], 0), axis=1)
    lower = (
        jnp.arange(tokens)[:, None] > jnp.arange(tokens)[None, :]
    ).astype(BF16)
    position = dot(lower, member.astype(BF16), ((1,), (0,))).astype(jnp.int32)
    hot = jnp.any(plan[:, None] == ids[None, :], axis=0)
    limit = capacity + spare * hot.astype(jnp.int32)
    position = jnp.where(member & (position < limit[None, :]), position, -1)
    slot = jnp.arange(width, dtype=jnp.int32)
    chosen = position[:, :, None] == slot[None, None, :]
    gates = jnp.where(chosen, gate[:, :, None], 0)
    chosen = chosen.reshape(tokens, experts * width)
    gates = gates.reshape(tokens, experts * width)
    return chosen.astype(BF16), gates


def on_device(tokens, routes, gate_fixed, counts, replica_plan, weight_in, weight_out, cotangent):
    token_count, features = tokens.shape
    top_count = routes.shape[1]
    groups = lax.axis_size("expert")
    experts = groups * weight_in.shape[0]
    capacity = 3 * token_count * top_count // (8 * experts)
    spare = capacity // 2
    width = capacity + spare
    chosen, gates = tables(
        routes, gate_fixed, counts[0], replica_plan, experts, capacity, spare
    )
    high = (gates // 256).astype(BF16)
    low = (gates % 256).astype(BF16)
    slot_scale = jnp.sum(gates, axis=0).astype(F32) / 65536.0
    sent = dot(chosen, tokens, ((0,), (0,))).astype(BF16).reshape(experts, width, features)
    grads = (dot(chosen, cotangent, ((0,), (0,))) * slot_scale[:, None]).astype(BF16)
    grads = grads.reshape(experts, width, features)
    w1 = weight_in[0]
    w2 = weight_out[0]

    def exchange(value):
        return lax.all_to_all(value, "expert", split_axis=0, concat_axis=0, tiled=True)

    rows = lax.all_gather(exchange(sent), "dp", axis=0, tiled=True).reshape(-1, features)
    grad = lax.all_gather(exchange(grads), "dp", axis=0, tiled=True).reshape(-1, features)
    pre = dot(rows, w1, ((1,), (0,)))
    act = activate(pre).astype(BF16)
    out = dot(act, w2, ((1,), (0,))).astype(BF16)
    out = out.reshape(-1, width, features)
    out = lax.psum_scatter(out, "dp", scatter_dimension=0, tiled=True)
    returned = exchange(out.astype(BF16)).reshape(-1, features)
    act_grad = dot(grad, w2, ((1,), (1,)))
    pre_grad = (act_grad * derivative(pre)).astype(BF16)
    dx = dot(pre_grad, w1, ((1,), (1,))).astype(BF16).reshape(-1, width, features)
    dx = lax.psum_scatter(dx, "dp", scatter_dimension=0, tiled=True)
    returned_dx = exchange(dx.astype(BF16)).reshape(-1, features)
    w2_grad = dot(act, grad, ((0,), (0,))).astype(BF16)[None]
    w1_grad = dot(rows, pre_grad, ((0,), (0,))).astype(BF16)[None]
    layer = dot(high, returned, ((1,), (0,))) * (1.0 / 256.0) + dot(
        low, returned, ((1,), (0,))
    ) * (1.0 / 65536.0)
    dx_sum = dot(chosen, returned_dx, ((1,), (0,)))
    return (layer.astype(BF16), dx_sum.astype(BF16), w1_grad, w2_grad)


def solution(mesh):
    both = P(("expert", "dp"), None)
    return jax.shard_map(
        on_device,
        mesh=mesh,
        in_specs=(
            both,
            both,
            both,
            P(("expert", "dp")),
            P(),
            P("expert", None, "dp"),
            P("expert", "dp", None),
            both,
        ),
        out_specs=(both, both, P("expert", None, "dp"), P("expert", "dp", None)),
        check_vma=False,
    )
```

```python
import jax
import jax.numpy as jnp
from jax import lax
from jax.experimental import pallas as pl
from jax.experimental.pallas import tpu as pltpu
from jax.sharding import PartitionSpec as P

F32 = jnp.float32
BF16 = jnp.bfloat16
MESH = pl.DeviceIdType.MESH


def activate(values):
    return values * jax.nn.sigmoid(1.702 * values)


def derivative(values):
    s = jax.nn.sigmoid(1.702 * values)
    return s + 1.702 * values * s * (1.0 - s)


def dot(a, b, dims):
    return lax.dot_general(a, b, (dims, ((), ())), preferred_element_type=F32)


def tables(routes, gate_fixed, live_count, plan, experts, capacity, spare, width):
    tokens = routes.shape[0]
    ids = jnp.arange(experts, dtype=jnp.int32)
    live = (jnp.arange(tokens, dtype=jnp.int32) < live_count)[:, None]
    same = routes[:, :, None] == ids[None, None, :]
    member = jnp.any(same, axis=1) & live
    gate = jnp.sum(jnp.where(same, gate_fixed[:, :, None], 0), axis=1)
    lower = (
        jnp.arange(tokens)[:, None] > jnp.arange(tokens)[None, :]
    ).astype(BF16)
    position = dot(lower, member.astype(BF16), ((1,), (0,))).astype(jnp.int32)
    hot = jnp.any(plan[:, None] == ids[None, :], axis=0)
    limit = capacity + spare * hot.astype(jnp.int32)
    position = jnp.where(member & (position < limit[None, :]), position, -1)
    slot = jnp.arange(width, dtype=jnp.int32)
    chosen = position[:, :, None] == slot[None, None, :]
    gates = jnp.where(chosen, gate[:, :, None], 0)
    chosen = chosen.reshape(tokens, experts * width)
    gates = gates.reshape(tokens, experts * width)
    return chosen.astype(BF16), gates


def places(experts):
    e = lax.axis_index("expert")
    d = lax.axis_index("dp")
    core = d % 2
    partner = d + 1 - 2 * core
    cross = (d + 2) % 4
    return e, d, core, partner, cross


def remote(src, dst, send, recv, target):
    return pltpu.make_async_remote_copy(
        src_ref=src,
        dst_ref=dst,
        send_sem=send,
        recv_sem=recv,
        device_id=target,
        device_id_type=MESH,
    )


def greet(experts, e, d, partner, cross):
    barrier = pltpu.get_barrier_semaphore()
    pl.semaphore_signal(barrier, inc=1, device_id=(e, partner), device_id_type=MESH)
    pl.semaphore_signal(barrier, inc=1, device_id=(e, cross), device_id_type=MESH)

    @pl.loop(1, experts)
    def _(k):
        pl.semaphore_signal(
            barrier, inc=1, device_id=((e + k) % experts, d), device_id_type=MESH
        )

    pl.semaphore_wait(barrier, experts + 1)


def inbound_kernel(
    experts, tok, grad, w1, w2, rows, grads, w1x, w2x,
    a_send, a_recv, c_send, c_recv, w_send, w_recv, own_sem,
):
    e, d, core, partner, cross = places(experts)
    greet(experts, e, d, partner, cross)
    sides = ((tok, rows), (grad, grads))
    weights = [
        remote(src, dst, w_send.at[i], w_recv.at[i], (e, cross))
        for i, (src, dst) in enumerate(((w1, w1x), (w2, w2x)))
    ]
    for copy in weights:
        copy.start()

    def across(j, k):
        src, dst = sides[j]
        target = (e + k) % experts
        return remote(
            src.at[target], dst.at[core, e], a_send.at[j, k], a_recv.at[j, k], (target, d)
        )

    def along(j, k):
        dst = sides[j][1]
        source = (e + experts - k) % experts
        return remote(
            dst.at[core, source],
            dst.at[core, source],
            c_send.at[j, k],
            c_recv.at[j, k],
            (e, partner),
        )

    owns = []
    for j in range(2):
        @pl.loop(1, experts)
        def _(k):
            across(j, k).start()

        own = pltpu.make_async_copy(sides[j][0].at[e], sides[j][1].at[core, e], own_sem.at[j])
        own.start()
        owns.append(own)
    for j in range(2):
        owns[j].wait()
        along(j, 0).start()

        @pl.loop(1, experts)
        def _(k):
            across(j, k).wait_recv()
            along(j, k).start()

    for j in range(2):
        @pl.loop(1, experts)
        def _(k):
            across(j, k).wait_send()

        @pl.loop(0, experts)
        def _(k):
            copy = along(j, k)
            copy.wait_send()
            copy.wait_recv()

    for copy in weights:
        copy.wait()


def outbound_kernel(
    experts, out, dx, g1, g2, ret, ret_dx, g1x, g2x,
    part, summed, a_send, a_recv, c_send, c_recv, w_send, w_recv,
):
    e, d, core, partner, cross = places(experts)
    greet(experts, e, d, partner, cross)
    sides = ((out, ret), (dx, ret_dx))

    def along(j, k):
        target = (e + k) % experts
        return remote(
            sides[j][0].at[1 - core, target],
            part.at[j, target],
            c_send.at[j, k],
            c_recv.at[j, k],
            (e, partner),
        )

    def across(j, k):
        target = (e + k) % experts
        return remote(
            summed.at[j, target],
            sides[j][1].at[e],
            a_send.at[j, k],
            a_recv.at[j, k],
            (target, d),
        )

    for j in range(2):
        @pl.loop(1, experts + 1)
        def _(k):
            along(j, k % experts).start()

    weights = [
        remote(src, dst, w_send.at[i], w_recv.at[i], (e, cross))
        for i, (src, dst) in enumerate(((g1, g1x), (g2, g2x)))
    ]
    for copy in weights:
        copy.start()

    for j in range(2):
        @pl.loop(1, experts)
        def _(k):
            along(j, k).wait_recv()
            target = (e + k) % experts
            total = sides[j][0][core, target].astype(F32) + part[j, target].astype(F32)
            summed[j, target] = total.astype(BF16)
            across(j, k).start()

        along(j, 0).wait_recv()
        total = sides[j][0][core, e].astype(F32) + part[j, e].astype(F32)
        sides[j][1][e] = total.astype(BF16)

    for j in range(2):
        @pl.loop(0, experts)
        def _(k):
            along(j, k).wait_send()

        @pl.loop(1, experts)
        def _(k):
            copy = across(j, k)
            copy.wait_send()
            copy.wait_recv()

    for copy in weights:
        copy.wait()


def inbound(experts, sent, grads, w1, w2):
    vm = pl.BlockSpec(memory_space=pltpu.VMEM)
    anywhere = pl.BlockSpec(memory_space=pl.ANY)
    dma = pltpu.SemaphoreType.DMA
    rows = jax.ShapeDtypeStruct((2,) + sent.shape, BF16)
    return pl.pallas_call(
        lambda *refs: inbound_kernel(experts, *refs),
        out_shape=(
            rows,
            rows,
            jax.ShapeDtypeStruct(w1.shape, BF16),
            jax.ShapeDtypeStruct(w2.shape, BF16),
        ),
        in_specs=[vm, vm, anywhere, anywhere],
        out_specs=(vm, vm, anywhere, anywhere),
        scratch_shapes=[dma((2, experts))] * 4 + [dma((2,))] * 3,
        compiler_params=pltpu.CompilerParams(collective_id=0, has_side_effects=True),
        name="inbound",
    )(sent, grads, w1, w2)


def outbound(experts, out, dx, g1, g2):
    vm = pl.BlockSpec(memory_space=pltpu.VMEM)
    anywhere = pl.BlockSpec(memory_space=pl.ANY)
    dma = pltpu.SemaphoreType.DMA
    rows = jax.ShapeDtypeStruct(out.shape[1:], BF16)
    return pl.pallas_call(
        lambda *refs: outbound_kernel(experts, *refs),
        out_shape=(
            rows,
            rows,
            jax.ShapeDtypeStruct(g1.shape, BF16),
            jax.ShapeDtypeStruct(g2.shape, BF16),
        ),
        in_specs=[vm, vm, anywhere, anywhere],
        out_specs=(vm, vm, anywhere, anywhere),
        scratch_shapes=[pltpu.VMEM((2,) + out.shape[1:], BF16)] * 2
        + [dma((2, experts))] * 4
        + [dma((2,))] * 2,
        compiler_params=pltpu.CompilerParams(collective_id=1, has_side_effects=True),
        name="outbound",
    )(out, dx, g1, g2)


def on_device(tokens, routes, gate_fixed, counts, replica_plan, weight_in, weight_out, cotangent):
    token_count, features = tokens.shape
    top_count = routes.shape[1]
    experts = lax.axis_size("expert") * weight_in.shape[0]
    capacity = 3 * token_count * top_count // (8 * experts)
    spare = capacity // 2
    width = -(-(capacity + spare) // 8) * 8
    chosen, gates = tables(
        routes, gate_fixed, counts[0], replica_plan, experts, capacity, spare, width
    )
    high = (gates // 256).astype(BF16)
    low = (gates % 256).astype(BF16)
    slot_scale = jnp.sum(gates, axis=0).astype(F32) / 65536.0
    sent = dot(chosen, tokens, ((0,), (0,))).astype(BF16).reshape(experts, width, features)
    grads = (dot(chosen, cotangent, ((0,), (0,))) * slot_scale[:, None]).astype(BF16)
    grads = grads.reshape(experts, width, features)
    w1 = weight_in[0]
    w2 = weight_out[0]
    rows, grad, w1x, w2x = inbound(experts, sent, grads, w1, w2)
    blocks = rows.shape
    rows = rows.reshape(-1, features)
    grad = grad.reshape(-1, features)

    def forward(first, second):
        pre = dot(rows, first, ((1,), (0,)))
        act = activate(pre).astype(BF16)
        act_grad = dot(grad, second, ((1,), (1,)))
        pre_grad = (act_grad * derivative(pre)).astype(BF16)
        g2 = dot(act, grad, ((0,), (0,)))
        g1 = dot(rows, pre_grad, ((0,), (0,)))
        return act, pre_grad, g1, g2

    act, pre_grad, g1, g2 = forward(w1, w2)
    act_x, pre_grad_x, g1_x, g2_x = forward(w1x, w2x)
    plain = ((1,), (0,))
    last = ((1,), (1,))
    out = (dot(act, w2, plain) + dot(act_x, w2x, plain)).astype(BF16)
    dx = (dot(pre_grad, w1, last) + dot(pre_grad_x, w1x, last)).astype(BF16)
    ret, ret_dx, g1_in, g2_in = outbound(
        experts, out.reshape(blocks), dx.reshape(blocks), g1_x.astype(BF16), g2_x.astype(BF16)
    )
    w1_grad = (g1 + g1_in.astype(F32)).astype(BF16)[None]
    w2_grad = (g2 + g2_in.astype(F32)).astype(BF16)[None]
    ret = ret.reshape(-1, features)
    ret_dx = ret_dx.reshape(-1, features)
    layer = dot(high, ret, plain) * (1.0 / 256.0) + dot(low, ret, plain) * (1.0 / 65536.0)
    dx_sum = dot(chosen, ret_dx, plain)
    return (layer.astype(BF16), dx_sum.astype(BF16), w1_grad, w2_grad)


def solution(mesh):
    both = P(("expert", "dp"), None)
    return jax.shard_map(
        on_device,
        mesh=mesh,
        in_specs=(
            both,
            both,
            both,
            P(("expert", "dp")),
            P(),
            P("expert", None, "dp"),
            P("expert", "dp", None),
            both,
        ),
        out_specs=(both, both, P("expert", None, "dp"), P("expert", "dp", None)),
        check_vma=False,
    )
```
